32 devices in a mesh: tm: 4 (over x, core), space: 8 (over z, y).
Axes of the slice: x: 2, y: 2, z: 4, core: 2. Of those that a mesh axis runs over, the one named last changes fastest.
Arguments:
- cotangent: bfloat16 [16, 64, 8192], P('tm', 'space'), may hold values from -6 to 6
- saved_mix: bfloat16 [16, 64, 8192], P('tm', 'space'), may hold values from -6 to 6
- saved_pre: bfloat16 [16, 64, 8192], P('tm', 'space'), may hold values from -8 to 8
- kernel_one: bfloat16 [4, 3, 3, 64, 64], replicated, may hold values from -0.25 to 0.25
- kernel_two: bfloat16 [4, 3, 3, 64, 64], replicated, may hold values from -0.25 to 0.25
- ref_pairs: int32 [16, 2], replicated, may hold values from 0 to 15, as said below
- frame_level: int32 [16], replicated, may hold values from 0 to 4, as said below
Outputs:
- input_grad: float32 [16, 64, 8192], P('tm', 'space')
- weight_grad_one: float32 [4, 3, 3, 64, 64], replicated
- weight_grad_two: float32 [4, 3, 3, 64, 64], replicated
The draws below stay inside these ranges and needn't reach their ends.
Inputs may be any that keep to these rules, and one draw needn't show every extreme that they name: Frame c was predicted from frames ref_pairs[c, 0] and ref_pairs[c, 1]; for a frame of level k >= 1 both have a level below k (at level 1 both name the level-0 frame); the level-0 frame names itself twice. `frame_level`: one frame has level 0 and 2**(k-1) frames have level k for k from 1 to 4; frames are stored in an order drawn from the seed.
All inputs are finite; a program needn't handle non-finite values.
Results may differ from the reference program's by a relative error of at most 0.006.
Values may be sent and summed in bfloat16 or wider, within the bound.
A program may use at most 64 MiB of HBM per device.

```python
import math
import jax
import jax.numpy as jnp
import numpy as np
from jax import lax

F = 16
LEVELS = 4
C = 64
W = 128
ROWS = 64


def gop_tables(key):
    storage = jax.random.permutation(jax.random.fold_in(key, 11), F).astype(jnp.int32)
    disp_level = np.zeros((F,), np.int32)
    disp_refs = np.zeros((F, 2), np.int32)
    for position in range(1, F):
        stride = position & -position
        disp_level[position] = LEVELS - (stride.bit_length() - 1)
        disp_refs[position, 0] = position - stride
        disp_refs[position, 1] = (position + stride) % F
    level_store = jnp.zeros((F,), jnp.int32).at[storage].set(jnp.asarray(disp_level))
    refs_store = jnp.zeros((F, 2), jnp.int32).at[storage].set(storage[jnp.asarray(disp_refs)])
    return (level_store, refs_store)


def draw_ref_pairs(key, part):
    return gop_tables(key)[1]


def draw_frame_level(key, part):
    return gop_tables(key)[0]


def block_levels(stream_key, shape, cuts, smallest, largest):
    def one(dim, blocks):
        heights = jax.random.uniform(jax.random.fold_in(jax.random.fold_in(stream_key, 6), dim), (blocks,), jnp.float32, smallest / len(cuts), largest / len(cuts))
        return jnp.repeat(jnp.exp(heights), shape[dim] // blocks).reshape((-1,) + (1,) * (len(shape) - dim - 1))

    loudness = one(*cuts[0])
    for cut in cuts[1:]:
        loudness = loudness * one(*cut)
    return loudness


def scatter_about(stream_key, shape, spread, limit, shards=(), kind=jnp.bfloat16):
    factor_of = block_levels(stream_key, shape, shards, -0.22, 0.18) if shards else 1.0
    entries = jax.random.normal(stream_key, shape, jnp.float32) * spread * factor_of
    return jnp.minimum(jnp.maximum(entries, -limit), limit).astype(kind)


def setup_inputs(seed: int = 0) -> dict:
    keys = jax.random.split(jax.random.key(seed), 8)
    return {
        "cotangent": scatter_about(keys[0], (F, ROWS, W * C), 1.0, 6.0, ((0, 4), (1, 8))),
        "saved_mix": scatter_about(keys[1], (F, ROWS, W * C), 1.0, 6.0, ((0, 4), (1, 8))),
        "saved_pre": scatter_about(keys[2], (F, ROWS, W * C), 1.5, 8.0, ((0, 4), (1, 8))),
        "kernel_one": scatter_about(keys[3], (LEVELS, 3, 3, C, C), (9 * C) ** -0.5, 0.25),
        "kernel_two": scatter_about(keys[4], (LEVELS, 3, 3, C, C), (9 * C) ** -0.5, 0.25),
        "ref_pairs": draw_ref_pairs(jax.random.fold_in(keys[7], 71), 0),
        "frame_level": draw_frame_level(jax.random.fold_in(keys[7], 71), 0),
    }


def shifted(field, row_tap, col_tap):
    padded = jnp.pad(field, ((0, 0), (1, 1), (1, 1), (0, 0)))
    return padded[:, row_tap:row_tap + ROWS, col_tap:col_tap + W]

def conv_full(field, kernel):
    running = jnp.zeros(field.shape[:3] + (C,), jnp.float32)
    for row_tap in range(3):
        for col_tap in range(3):
            moved = shifted(field, row_tap, col_tap).reshape(-1, C)
            running = running + jnp.dot(moved, kernel[row_tap, col_tap], preferred_element_type=jnp.float32).reshape(running.shape)
    return running

def adjoint(field, kernel):
    return conv_full(field, jnp.transpose(kernel[::-1, ::-1], (0, 1, 3, 2)))

def correlate_full(field, cot):
    cot_wide = cot.astype(jnp.float32)
    rows_out = []
    for row_tap in range(3):
        taps = []
        for col_tap in range(3):
            moved = shifted(field, row_tap, col_tap).astype(jnp.float32)
            taps.append(jnp.einsum('frwi,frwo->fio', moved, cot_wide, precision=lax.Precision.HIGHEST))
        rows_out.append(jnp.stack(taps, axis=1))
    return jnp.stack(rows_out, axis=1)

def reference(cotangent, saved_mix, saved_pre, kernel_one, kernel_two, ref_pairs, frame_level):
    shape_four = (F, ROWS, W, C)
    preact = saved_pre.astype(jnp.float32).reshape(shape_four)
    sigmoid_pre = jax.nn.sigmoid(preact)
    act_slope = sigmoid_pre * (1.0 + preact * (1.0 - sigmoid_pre))
    act_out = (preact * sigmoid_pre).astype(jnp.bfloat16)
    cot_total = cotangent.astype(jnp.float32).reshape(shape_four)
    kept_grad = jnp.zeros(shape_four, jnp.bfloat16)
    frame_ids = jnp.arange(F, dtype=jnp.int32)
    for level_now in range(LEVELS, 0, -1):
        chosen = jnp.nonzero(frame_level == level_now, size=2 ** (level_now - 1))[0].astype(jnp.int32)
        cot_round = cot_total[chosen].astype(jnp.bfloat16)
        slot_grad = (adjoint(cot_round, kernel_two[level_now - 1]) * act_slope[chosen]).astype(jnp.bfloat16)
        to_refs = adjoint(slot_grad, kernel_one[level_now - 1]).astype(jnp.bfloat16)
        kept_grad = kept_grad.at[chosen].set(slot_grad)
        first_ref = ref_pairs[chosen, 0]
        second_ref = ref_pairs[chosen, 1]
        weights = 0.5 * ((first_ref[:, None] == frame_ids[None, :]).astype(jnp.float32) + (second_ref[:, None] == frame_ids[None, :]).astype(jnp.float32))
        added = jnp.dot(weights.T.astype(jnp.bfloat16), to_refs.reshape(to_refs.shape[0], -1), preferred_element_type=jnp.float32)
        cot_total = cot_total + added.reshape(shape_four)
    final_cot = cot_total.astype(jnp.bfloat16)
    level_hot = (frame_level[:, None] == jnp.arange(1, LEVELS + 1, dtype=jnp.int32)[None, :]).astype(jnp.float32)
    scale = 1.0 / math.sqrt(ROWS * W)
    mix_four = saved_mix.reshape(shape_four)
    per_one = correlate_full(mix_four, kept_grad)
    per_two = correlate_full(act_out, final_cot)
    grad_one = scale * lax.optimization_barrier(jnp.sum(level_hot[:, :, None, None, None, None] * per_one[:, None], axis=0))
    grad_two = scale * lax.optimization_barrier(jnp.sum(level_hot[:, :, None, None, None, None] * per_two[:, None], axis=0))
    return (cot_total.reshape(F, ROWS, W * C), grad_one, grad_two)
```

```python
import functools
import math

import jax
import jax.numpy as jnp
from jax import lax
from jax.experimental import pallas as pl
from jax.experimental.pallas import tpu as pltpu
from jax.sharding import PartitionSpec as P


def reduce_kernel(nx, ns, g_ref, out_ref, send1, got1, send2, got2, send3, got3, whole, ssem, rsem):
    tm = lax.axis_index("tm")
    core = tm % 2
    xi = tm // 2
    sp = lax.axis_index("space")

    def peer(kind, step):
        if kind == 0:
            return (xi * 2 + (1 - core), sp)
        if kind == 1:
            return (((xi + step) % nx) * 2 + core, sp)
        return (tm, (sp + step) % ns)

    peers = [(0, 1)] + [(1, d) for d in range(1, nx)] + [(2, d) for d in range(1, ns)]
    barrier = pltpu.get_barrier_semaphore()
    for kind, step in peers:
        pl.semaphore_signal(
            barrier, inc=1, device_id=peer(kind, step), device_id_type=pl.DeviceIdType.MESH
        )
    pl.semaphore_wait(barrier, len(peers))

    def send(src, dst, slot, kind, step):
        copy = pltpu.make_async_remote_copy(
            src_ref=src,
            dst_ref=dst,
            send_sem=ssem.at[slot],
            recv_sem=rsem.at[slot],
            device_id=peer(kind, step),
            device_id_type=pl.DeviceIdType.MESH,
        )
        copy.start()
        return copy

    send1[...] = g_ref[1 - core].astype(jnp.bfloat16)
    slot = 0
    copy = send(send1, got1, slot, 0, 1)
    slot += 1
    copy.wait()
    total = g_ref[core] + got1[...].astype(jnp.float32)
    send2[...] = total.astype(jnp.bfloat16)
    copies = []
    for d in range(1, nx):
        copies.append(send(send2.at[(xi + d) % nx], got2.at[d - 1], slot, 1, d))
        slot += 1
    for copy in copies:
        copy.wait()
    part = send2[xi].astype(jnp.float32)
    for d in range(1, nx):
        part = part + got2[d - 1].astype(jnp.float32)
    send3[...] = part.astype(jnp.bfloat16)
    copies = []
    for d in range(1, ns):
        copies.append(send(send3.at[(sp + d) % ns], got3.at[d - 1], slot, 2, d))
        slot += 1
    for copy in copies:
        copy.wait()
    mine = send3[sp].astype(jnp.float32)
    for d in range(1, ns):
        mine = mine + got3[d - 1].astype(jnp.float32)
    whole[core, xi, sp] = mine.astype(jnp.bfloat16)
    copies = []
    for d in range(1, ns):
        copies.append(send(whole.at[core, xi, sp], whole.at[core, xi, sp], slot, 2, d))
        slot += 1
    for copy in copies:
        copy.wait()
    copies = []
    for d in range(1, nx):
        copies.append(send(whole.at[core, xi], whole.at[core, xi], slot, 1, d))
        slot += 1
    for copy in copies:
        copy.wait()
    send(whole.at[core], whole.at[core], slot, 0, 1).wait()
    out_ref[...] = whole[...].astype(jnp.float32)


def reduce_all(flat):
    nx = lax.axis_size("tm") // 2
    ns = lax.axis_size("space")
    rows = flat.shape[0] // (2 * nx * ns)
    body = (nx, ns, rows, 128)
    bf = jnp.bfloat16
    count = 2 * (1 + nx - 1 + ns - 1)
    vmem = pl.BlockSpec(memory_space=pltpu.VMEM)
    out = pl.pallas_call(
        functools.partial(reduce_kernel, nx, ns),
        out_shape=jax.ShapeDtypeStruct((2,) + body, jnp.float32),
        in_specs=[vmem],
        out_specs=vmem,
        scratch_shapes=[
            pltpu.VMEM(body, bf),
            pltpu.VMEM(body, bf),
            pltpu.VMEM(body, bf),
            pltpu.VMEM((max(nx - 1, 1),) + body[1:], bf),
            pltpu.VMEM(body[1:], bf),
            pltpu.VMEM((max(ns - 1, 1),) + body[2:], bf),
            pltpu.VMEM((2,) + body, bf),
            pltpu.SemaphoreType.DMA((count,)),
            pltpu.SemaphoreType.DMA((count,)),
        ],
        compiler_params=pltpu.CompilerParams(
            collective_id=7, has_side_effects=True, vmem_limit_bytes=40 * 2**20
        ),
        name="reduce_all",
    )(flat.reshape((2,) + body))
    return out.reshape(flat.shape)


def padded_2(cells, sides, width):
    for axis, dim in sides:
        count = lax.axis_size(axis)
        ends = count - 1
        head = lax.slice_in_dim(cells, 0, width, axis=dim)
        tail = lax.slice_in_dim(cells, cells.shape[dim] - width, cells.shape[dim], axis=dim)
        cells = jnp.concatenate(
            [
                lax.ppermute(tail, axis, [(i, (i + 1) % count) for i in range(ends)]),
                cells,
                lax.ppermute(head, axis, [((i + 1) % count, i) for i in range(ends)]),
            ],
            axis=dim,
        )
    return cells


def flipped(kernel):
    return jnp.transpose(kernel[::-1, ::-1], (0, 1, 3, 2))


def pair_kernel(kernel):
    blank = jnp.zeros_like(kernel[:, 0])
    row_blocks = []
    for in_part in range(4):
        col_blocks = []
        for out_half in range(2):
            col_tap = in_part - out_half
            col_blocks.append(kernel[:, col_tap] if 0 <= col_tap <= 2 else blank)
        row_blocks.append(jnp.concatenate(col_blocks, axis=-1))
    return jnp.concatenate(row_blocks, axis=1)


def pair_view(field, channels):
    col_count = field.shape[2] // channels
    grid = field.reshape(field.shape[0], field.shape[1], col_count, channels)
    grid = jnp.pad(grid, ((0, 0), (0, 0), (1, 1), (0, 0)))
    grid = grid.reshape(field.shape[0], field.shape[1], (col_count + 2) // 2, 2 * channels)
    return jnp.concatenate((grid[:, :, :-1], grid[:, :, 1:]), axis=-1)


def conv_taps(field, paired):
    channels = paired.shape[2] // 2
    windows = pair_view(field, channels)
    row_count = field.shape[1] - 2
    result = jnp.einsum(
        "nrjk,kc->nrjc", windows[:, 0:row_count], paired[0], preferred_element_type=jnp.float32
    )
    for row_tap in range(1, 3):
        result = result + jnp.einsum(
            "nrjk,kc->nrjc",
            windows[:, row_tap : row_tap + row_count],
            paired[row_tap],
            preferred_element_type=jnp.float32,
        )
    return result.reshape(field.shape[0], row_count, -1)


def correlate(field, cot, channels):
    windows = pair_view(field, channels)
    row_count = cot.shape[1]
    cot_pairs = cot.reshape(cot.shape[0], row_count, -1, 2 * channels)
    taps = []
    for row_tap in range(3):
        blocks = jnp.einsum(
            "nrjk,nrjc->nkc",
            windows[:, row_tap : row_tap + row_count],
            cot_pairs,
            preferred_element_type=jnp.float32,
        )
        row_taps = []
        for col_tap in range(3):
            first_part = blocks[:, col_tap * channels : (col_tap + 1) * channels, 0:channels]
            second_part = blocks[
                :, (col_tap + 1) * channels : (col_tap + 2) * channels, channels : 2 * channels
            ]
            row_taps.append(first_part + second_part)
        taps.append(jnp.stack(row_taps, axis=1))
    return jnp.stack(taps, axis=1)


def backprop(slot_cot, slot_slope, kernel_inner, kernel_outer):
    padded = padded_2(slot_cot, (("space", 1),), 1)
    slot_grad = (conv_taps(padded, kernel_inner) * slot_slope).astype(jnp.bfloat16)
    grad_padded = padded_2(slot_grad, (("space", 1),), 1)
    to_refs = conv_taps(grad_padded, kernel_outer).astype(jnp.bfloat16)
    return (slot_grad, to_refs)


def body_time(cotangent, saved_mix, saved_pre, kernel_one, kernel_two, ref_pairs, frame_level):
    frames_dev = cotangent.shape[0]
    row_count = cotangent.shape[1]
    channels = kernel_one.shape[-1]
    levels_all = kernel_one.shape[0]
    col_count = cotangent.shape[2] // channels
    first_frame = lax.axis_index("tm") * frames_dev
    local_ids = first_frame + jnp.arange(frames_dev, dtype=jnp.int32)
    local_level = lax.dynamic_slice_in_dim(frame_level, first_frame, frames_dev, 0)
    frame_count = ref_pairs.shape[0]
    all_frames = jnp.arange(frame_count, dtype=jnp.int32)
    preact = saved_pre.astype(jnp.float32)
    sigmoid_pre = jax.nn.sigmoid(preact)
    act_slope = sigmoid_pre * (1.0 + preact * (1.0 - sigmoid_pre))
    act_out = (preact * sigmoid_pre).astype(jnp.bfloat16)
    saved_rims = padded_2(jnp.stack((saved_mix, act_out)), (("space", 2),), 1)
    cot_total = cotangent.astype(jnp.float32)
    kept_grad = jnp.zeros_like(cotangent)
    for level_now in range(levels_all, 0, -1):
        active = local_level == level_now
        slot_count = min(frames_dev, 2 ** (level_now - 1))
        ranks = jnp.cumsum(active.astype(jnp.int32)) - 1
        picker = jnp.logical_and(
            ranks[None, :] == jnp.arange(slot_count, dtype=jnp.int32)[:, None], active[None, :]
        )
        picker_wide = picker.astype(jnp.float32)
        slot_cot = jnp.einsum(
            "sf,fx->sx",
            picker.astype(jnp.bfloat16),
            cot_total.astype(jnp.bfloat16).reshape(frames_dev, -1),
            preferred_element_type=jnp.float32,
        )
        slot_cot = slot_cot.astype(jnp.bfloat16).reshape(slot_count, row_count, -1)
        slot_slope = jnp.einsum(
            "sf,fx->sx",
            picker_wide,
            act_slope.reshape(frames_dev, -1),
            precision=lax.Precision.HIGHEST,
        ).reshape(slot_count, row_count, -1)
        slot_ids = jnp.sum(picker.astype(jnp.int32) * local_ids[None, :], axis=1)
        slot_ok = jnp.sum(picker.astype(jnp.int32), axis=1)
        kernel_inner = pair_kernel(flipped(kernel_two[level_now - 1]))
        kernel_outer = pair_kernel(flipped(kernel_one[level_now - 1]))
        slot_grad, to_refs = backprop(slot_cot, slot_slope, kernel_inner, kernel_outer)
        frame_grad = jnp.einsum(
            "sf,sx->fx",
            picker.astype(jnp.bfloat16),
            slot_grad.reshape(slot_grad.shape[0], -1),
            preferred_element_type=jnp.float32,
        )
        frame_grad = frame_grad.astype(jnp.bfloat16).reshape(kept_grad.shape)
        kept_grad = jnp.where(active[:, None, None], frame_grad, kept_grad)
        moved = lax.all_gather(to_refs, "tm", axis=0, tiled=True)
        sender_ids = lax.all_gather(slot_ids, "tm", axis=0, tiled=True)
        sender_ok = lax.all_gather(slot_ok, "tm", axis=0, tiled=True)
        matches = (sender_ids[:, None] == all_frames[None, :]).astype(jnp.int32)
        first_ref = jnp.sum(matches * ref_pairs[None, :, 0], axis=1)
        second_ref = jnp.sum(matches * ref_pairs[None, :, 1], axis=1)
        hits = (first_ref[:, None] == local_ids[None, :]).astype(jnp.float32) + (
            second_ref[:, None] == local_ids[None, :]
        ).astype(jnp.float32)
        weights = 0.5 * sender_ok[:, None].astype(jnp.float32) * hits
        added = jnp.einsum(
            "kf,kx->fx",
            weights.astype(jnp.bfloat16),
            moved.reshape(moved.shape[0], -1),
            preferred_element_type=jnp.float32,
        )
        cot_total = cot_total + added.reshape(cot_total.shape)
    final_cot = cot_total.astype(jnp.bfloat16)
    per_one = correlate(saved_rims[0], kept_grad, channels)
    per_two = correlate(saved_rims[1], final_cot, channels)
    level_hot = (
        local_level[:, None] == jnp.arange(1, levels_all + 1, dtype=jnp.int32)[None, :]
    ).astype(jnp.float32)
    scale = 1.0 / math.sqrt(row_count * lax.axis_size("space") * col_count)
    sum_one = scale * jnp.sum(level_hot[:, :, None, None, None, None] * per_one[:, None], axis=0)
    sum_two = scale * jnp.sum(level_hot[:, :, None, None, None, None] * per_two[:, None], axis=0)
    flat = jnp.stack((sum_one, sum_two)).reshape(-1, 128)
    both = reduce_all(flat).reshape((2,) + sum_one.shape)
    weight_one, weight_two = both[0], both[1]
    return (cot_total, weight_one, weight_two)


def on_device(cotangent, saved_mix, saved_pre, kernel_one, kernel_two, ref_pairs, frame_level):
    return body_time(
        cotangent, saved_mix, saved_pre, kernel_one, kernel_two, ref_pairs, frame_level
    )


def solution(mesh):
    placed = (
        P("tm", "space", None),
        P("tm", "space", None),
        P("tm", "space", None),
        P(),
        P(),
        P(),
        P(),
    )
    return jax.shard_map(
        on_device,
        mesh=mesh,
        in_specs=placed,
        out_specs=(P("tm", "space", None), P(), P()),
        check_vma=False,
    )
```

```python
import functools
import math

import jax
import jax.numpy as jnp
from jax import lax
from jax.experimental import pallas as pl
from jax.experimental.pallas import tpu as pltpu
from jax.sharding import PartitionSpec as P


def reduce_kernel(nx, ns, g_ref, out_ref, send1, got1, send2, got2, send3, got3, whole, ssem, rsem):
    tm = lax.axis_index("tm")
    core = tm % 2
    xi = tm // 2
    sp = lax.axis_index("space")

    def peer(kind, step):
        if kind == 0:
            return (xi * 2 + (1 - core), sp)
        if kind == 1:
            return (((xi + step) % nx) * 2 + core, sp)
        return (tm, (sp + step) % ns)

    peers = [(0, 1)] + [(1, d) for d in range(1, nx)] + [(2, d) for d in range(1, ns)]
    barrier = pltpu.get_barrier_semaphore()
    for kind, step in peers:
        pl.semaphore_signal(
            barrier, inc=1, device_id=peer(kind, step), device_id_type=pl.DeviceIdType.MESH
        )
    pl.semaphore_wait(barrier, len(peers))

    def send(src, dst, slot, kind, step):
        copy = pltpu.make_async_remote_copy(
            src_ref=src,
            dst_ref=dst,
            send_sem=ssem.at[slot],
            recv_sem=rsem.at[slot],
            device_id=peer(kind, step),
            device_id_type=pl.DeviceIdType.MESH,
        )
        copy.start()
        return copy

    send1[...] = g_ref[1 - core].astype(jnp.bfloat16)
    slot = 0
    copy = send(send1, got1, slot, 0, 1)
    slot += 1
    copy.wait()
    total = g_ref[core] + got1[...].astype(jnp.float32)
    send2[...] = total.astype(jnp.bfloat16)
    copies = []
    for d in range(1, nx):
        copies.append(send(send2.at[(xi + d) % nx], got2.at[d - 1], slot, 1, d))
        slot += 1
    for copy in copies:
        copy.wait()
    part = send2[xi].astype(jnp.float32)
    for d in range(1, nx):
        part = part + got2[d - 1].astype(jnp.float32)
    send3[...] = part.astype(jnp.bfloat16)
    copies = []
    for d in range(1, ns):
        copies.append(send(send3.at[(sp + d) % ns], got3.at[d - 1], slot, 2, d))
        slot += 1
    for copy in copies:
        copy.wait()
    mine = send3[sp].astype(jnp.float32)
    for d in range(1, ns):
        mine = mine + got3[d - 1].astype(jnp.float32)
    whole[core, xi, sp] = mine.astype(jnp.bfloat16)
    copies = []
    for d in range(1, ns):
        copies.append(send(whole.at[core, xi, sp], whole.at[core, xi, sp], slot, 2, d))
        slot += 1
    for copy in copies:
        copy.wait()
    copies = []
    for d in range(1, nx):
        copies.append(send(whole.at[core, xi], whole.at[core, xi], slot, 1, d))
        slot += 1
    for copy in copies:
        copy.wait()
    send(whole.at[core], whole.at[core], slot, 0, 1).wait()
    out_ref[...] = whole[...].astype(jnp.float32)


def reduce_all(flat):
    nx = lax.axis_size("tm") // 2
    ns = lax.axis_size("space")
    rows = flat.shape[0] // (2 * nx * ns)
    body = (nx, ns, rows, 128)
    bf = jnp.bfloat16
    count = 2 * (1 + nx - 1 + ns - 1)
    vmem = pl.BlockSpec(memory_space=pltpu.VMEM)
    out = pl.pallas_call(
        functools.partial(reduce_kernel, nx, ns),
        out_shape=jax.ShapeDtypeStruct((2,) + body, jnp.float32),
        in_specs=[vmem],
        out_specs=vmem,
        scratch_shapes=[
            pltpu.VMEM(body, bf),
            pltpu.VMEM(body, bf),
            pltpu.VMEM(body, bf),
            pltpu.VMEM((max(nx - 1, 1),) + body[1:], bf),
            pltpu.VMEM(body[1:], bf),
            pltpu.VMEM((max(ns - 1, 1),) + body[2:], bf),
            pltpu.VMEM((2,) + body, bf),
            pltpu.SemaphoreType.DMA((count,)),
            pltpu.SemaphoreType.DMA((count,)),
        ],
        compiler_params=pltpu.CompilerParams(
            collective_id=7, has_side_effects=True, vmem_limit_bytes=40 * 2**20
        ),
        name="reduce_all",
    )(flat.reshape((2,) + body))
    return out.reshape(flat.shape)


BF = jnp.bfloat16
F32 = jnp.float32


def group_kernel(nt, ns, levels, cot_ref, pre_ref, mix_ref, perm_ref, back_ref, comb_ref, inner_ref,
                 outer_ref, grad_ref, one_ref, two_ref, raw, edge_s, edge_r, hal_s, hal_r, cot, pre,
                 mix, act, slope, kept, work, refs, im, conv_out, out_s, out_r, rhs_buf, ssem, rsem):
    tm = lax.axis_index("tm")
    sp = lax.axis_index("space")
    fl, rows, _ = cot_ref.shape
    frames = fl * nt
    lanes = cot.shape[2]
    own = lanes - 1536
    span = own + 1024
    mid = slice(256, 256 + span)
    quads = lanes // 256
    inner_q = quads - 2
    down = (sp + 1) % ns
    up = (sp + ns - 1) % ns

    barrier = pltpu.get_barrier_semaphore()
    peers = [((tm + d) % nt, sp) for d in range(1, nt)] + [(tm, up), (tm, down)]
    for peer in peers:
        pl.semaphore_signal(barrier, inc=1, device_id=peer, device_id_type=pl.DeviceIdType.MESH)
    pl.semaphore_wait(barrier, len(peers))
    slots = [0]

    def send(src, dst, peer):
        copy = pltpu.make_async_remote_copy(
            src_ref=src, dst_ref=dst, send_sem=ssem.at[slots[0]], recv_sem=rsem.at[slots[0]],
            device_id=peer, device_id_type=pl.DeviceIdType.MESH)
        copy.start()
        slots[0] += 1
        return copy

    sources = (cot_ref, pre_ref, mix_ref)
    waits = []
    for n in range(3):
        group = []
        for d in range(1, nt):
            to = (tm + d) % nt
            window = pl.ds(pl.multiple_of(to * own, 128), span)
            group.append(send(sources[n].at[:, :, window], raw.at[n, tm], (to, sp)))
        waits.append(group)
    mine = pl.ds(pl.multiple_of(tm * own, 128), span)
    for n in range(3):
        raw[n, tm] = sources[n][:, :, mine]
    perm = perm_ref[...]
    targets = (cot, pre, mix)
    for n in range(3):
        for copy in waits[n]:
            copy.wait()
        targets[n][...] = jnp.zeros_like(targets[n])
        for j in range(inner_q):
            cut = slice(256 * j, 256 * j + 256)
            block = raw[n, :, :, :, cut].astype(F32).reshape(frames * rows, 256).astype(BF)
            moved = jnp.dot(perm, block, preferred_element_type=F32)
            targets[n][2 : 2 + rows, :, 256 * j + 256 : 256 * j + 512] = moved.reshape(rows, frames, 256)
    halos = []
    for n in range(2):
        held = targets[1 + n]
        edge_s[n, 0] = held[2, :, mid].astype(BF)
        edge_s[n, 1] = held[rows + 1, :, mid].astype(BF)
        halos.append(send(edge_s.at[n, 0], edge_r.at[n, 1], (tm, up)))
        halos.append(send(edge_s.at[n, 1], edge_r.at[n, 0], (tm, down)))

    def push(k):
        g = 0 if k == levels - 1 else 8
        hal_s[k, 0] = cot[2:4, g : g + 8, mid].reshape(16, span).astype(BF)
        hal_s[k, 1] = cot[rows : rows + 2, g : g + 8, mid].reshape(16, span).astype(BF)
        return [send(hal_s.at[k, 0], hal_r.at[k, 1], (tm, up)),
                send(hal_s.at[k, 1], hal_r.at[k, 0], (tm, down))]

    flight = push(levels - 1)
    for copy in halos:
        copy.wait()
    has_up = (sp > 0).astype(F32)
    has_down = (sp < ns - 1).astype(F32)
    for n in range(2):
        held = targets[1 + n]
        held[1, :, mid] = edge_r[n, 0].astype(F32) * has_up
        held[rows + 2, :, mid] = edge_r[n, 1].astype(F32) * has_down
    column = lax.broadcasted_iota(jnp.int32, (8, lanes), 1) + tm * own - 768
    inside = jnp.logical_and(column >= 0, column < own * nt).astype(F32)
    for r in range(rows + 2):
        gate = has_up if r == 0 else (has_down if r == rows + 1 else 1.0)
        for g in (0, 8):
            v = pre[r + 1, g : g + 8]
            sig = jax.nn.sigmoid(v)
            slope[r, g : g + 8] = sig * (1.0 + v * (1.0 - sig)) * inside * gate
            act[r + 1, g : g + 8] = v * sig

    def fill(source, g, first, count, base, width):
        for r in range(count):
            for j in range(0, width, 2):
                lo = 256 * (base + j) - 128
                one = source[first + r, g : g + 8, lo : lo + 512]
                two = source[first + r, g : g + 8, lo + 256 : lo + 768]
                im[r, 8 * j : 8 * j + 16] = jnp.concatenate((one, two), axis=0).astype(BF)

    def conv(weights_ref, k, count, store):
        half = count // 2
        for part in range(2):
            total = None
            for a in range(3):
                lhs = im[part * half + a : part * half + a + half].reshape(half * 8 * inner_q, 512)
                term = jnp.dot(lhs, weights_ref[k, a], preferred_element_type=F32)
                total = term if total is None else total + term
            conv_out[0 : half * 8 * inner_q] = total
            for r in range(half):
                for j in range(inner_q):
                    at = (r * inner_q + j) * 8
                    store(part * half + r, j + 1, conv_out[at : at + 8])

    kept[...] = jnp.zeros_like(kept)
    work[...] = jnp.zeros_like(work)
    slot_no = lax.broadcasted_iota(jnp.int32, (8, 256), 0) + 8
    for k in range(levels - 1, -1, -1):
        g = 0 if k == levels - 1 else 8
        for copy in flight:
            copy.wait()
        cot[0:2, g : g + 8, mid] = hal_r[k, 0].astype(F32).reshape(2, 8, span) * has_up
        cot[rows + 2 : rows + 4, g : g + 8, mid] = (
            hal_r[k, 1].astype(F32).reshape(2, 8, span) * has_down)
        lowest = frames - 2 ** (k + 1)
        active = jnp.logical_and(slot_no >= lowest, slot_no < lowest + 2**k)

        def put_grad(r, j, block):
            cut = slice(256 * j, 256 * j + 256)
            value = (block * slope[r, g : g + 8, cut]).astype(BF).astype(F32)
            work[r, :, cut] = value
            if 1 <= r <= rows:
                if g:
                    value = jnp.where(active, value, kept[r - 1, g : g + 8, cut])
                kept[r - 1, g : g + 8, cut] = value

        fill(cot, g, 0, rows + 4, 1, inner_q)
        conv(inner_ref, k, rows + 2, put_grad)

        def put_refs(r, j, block):
            cut = slice(256 * j, 256 * j + 256)
            refs[r, :, cut] = block * inside[:, cut]

        fill(work, 0, 0, rows + 2, 1, inner_q)
        conv(outer_ref, k, rows, put_refs)
        for j in range(1, quads - 1):
            cut = slice(256 * j, 256 * j + 256)
            rhs = refs[0:rows, :, cut].reshape(rows * 8, 256).astype(BF)
            extra = jnp.dot(comb_ref[k], rhs, preferred_element_type=F32)
            cot[2 : 2 + rows, :, cut] += extra.reshape(rows, frames, 256)
        if k > 0:
            flight = push(k - 1)
    back = back_ref[...]
    outs = []
    for j in range(own // 256):
        cut = slice(768 + 256 * j, 1024 + 256 * j)
        flat = cot[2 : 2 + rows, :, cut].reshape(rows * frames, 256).astype(BF)
        moved = jnp.dot(back, flat, preferred_element_type=F32).astype(BF)
        out_s[:, :, 256 * j : 256 * j + 256] = moved.reshape(nt, fl * rows, 256)
    for d in range(1, nt):
        to = (tm + d) % nt
        outs.append(send(out_s.at[to], out_r.at[tm], (to, sp)))
    out_r[tm] = out_s[tm]

    wide = own // 256
    for n in range(2):
        source = (mix, act)[n]
        other = (kept, cot)[n]
        result = (one_ref, two_ref)[n]
        low = (0, 2)[n]
        for g in (0, 8):
            fill(source, g, 1, rows + 2, 3, wide)
            tall = 8 * wide
            for k in range(levels):
                if (k == levels - 1) != (g == 0):
                    continue
                lowest = frames - 2 ** (k + 1)
                active = jnp.logical_and(slot_no >= lowest, slot_no < lowest + 2**k)
                for r in range(rows):
                    for j in range(0, wide, 2):
                        cut = 768 + 256 * j
                        left = other[low + r, g : g + 8, cut : cut + 256]
                        right = other[low + r, g : g + 8, cut + 256 : cut + 512]
                        if g:
                            left = jnp.where(active, left, 0.0)
                            right = jnp.where(active, right, 0.0)
                        rhs_buf[r, 8 * j : 8 * j + 16] = jnp.concatenate(
                            (left, right), axis=0).astype(BF)
                rhs = rhs_buf[...].reshape(rows * tall, 256)
                for a in range(3):
                    lhs = im[a : a + rows, 0:tall].reshape(rows * tall, 512)
                    block = lax.dot_general(
                        lhs, rhs, (((0,), (0,)), ((), ())), preferred_element_type=F32)
                    taps = block[64:256, 0:64]
                    for p in range(1, 4):
                        taps = taps + block[64 * (p + 1) : 64 * (p + 4), 64 * p : 64 * p + 64]
                    result[k, a] = taps * (1.0 / math.sqrt(rows * ns * (own * nt // 64)))
    for copy in outs:
        copy.wait()
    for d in range(nt):
        grad_ref[:, own * d : own * d + own] = out_r[d].astype(F32)


def banded(kernel):
    hot = jnp.stack([jnp.eye(8, 4, k=-(b + 1), dtype=kernel.dtype) for b in range(3)])
    wide = jnp.einsum("labio,bqp->laqipo", kernel, hot)
    return wide.reshape(kernel.shape[0], 3, 512, 256)


def on_device(cotangent, saved_mix, saved_pre, kernel_one, kernel_two, ref_pairs, frame_level):
    fl, rows, width = cotangent.shape
    nt = lax.axis_size("tm")
    ns = lax.axis_size("space")
    levels = kernel_one.shape[0]
    frames = fl * nt
    own = width // nt
    lanes = own + 1536
    span = own + 1024
    quads = lanes // 256
    ids = jnp.arange(frames, dtype=jnp.int32)
    order = (levels - frame_level) * frames + ids
    rank = jnp.sum((order[None, :] < order[:, None]).astype(jnp.int32), axis=1)
    hot = (rank[None, :] == ids[:, None]).astype(F32)
    eye = jnp.eye(rows, dtype=F32)
    perm = (hot[None, :, :, None] * eye[:, None, None, :]).reshape(rows * frames, rows * frames)
    perm = perm.astype(BF)
    back = (hot.T[:, None, None, :] * eye[None, :, :, None]).reshape(rows * frames, rows * frames)
    back = back.astype(BF)
    ref_hot = 0.5 * jnp.sum((ref_pairs[:, :, None] == ids[None, None, :]).astype(F32), axis=1)
    mixw = jnp.einsum("tf,cf,sc->ts", hot, ref_hot, hot, precision=lax.Precision.HIGHEST)
    combs = []
    for k in range(levels):
        g = 0 if k == levels - 1 else 8
        lowest = frames - 2 ** (k + 1)
        on = jnp.logical_and(ids >= lowest, ids < lowest + 2**k).astype(F32)
        part = (mixw * on[None, :])[:, g : g + 8]
        combs.append((eye[:, None, :, None] * part[None, :, None, :]).reshape(
            rows * frames, rows * 8))
    comb = jnp.stack(combs).astype(BF)
    flip = lambda kernel: jnp.swapaxes(kernel[:, ::-1, ::-1], 3, 4)
    inner = banded(flip(kernel_two))
    outer = banded(flip(kernel_one))
    pads = ((0, 0), (0, 0), (512, 512))
    vmem = pl.BlockSpec(memory_space=pltpu.VMEM)
    count = 3 * (nt - 1) + 4 + 2 * levels + nt - 1
    tall = rows + 4
    grad, one, two = pl.pallas_call(
        functools.partial(group_kernel, nt, ns, levels),
        out_shape=(
            jax.ShapeDtypeStruct((fl * rows, width), F32),
            jax.ShapeDtypeStruct((levels, 3, 192, 64), F32),
            jax.ShapeDtypeStruct((levels, 3, 192, 64), F32),
        ),
        in_specs=[vmem] * 8,
        out_specs=(vmem, vmem, vmem),
        scratch_shapes=[
            pltpu.VMEM((3, nt, fl, rows, span), BF),
            pltpu.VMEM((2, 2, frames, span), BF),
            pltpu.VMEM((2, 2, frames, span), BF),
            pltpu.VMEM((levels, 2, 16, span), BF),
            pltpu.VMEM((levels, 2, 16, span), BF),
            pltpu.VMEM((tall, frames, lanes), F32),
            pltpu.VMEM((tall, frames, lanes), F32),
            pltpu.VMEM((tall, frames, lanes), F32),
            pltpu.VMEM((tall, frames, lanes), F32),
            pltpu.VMEM((rows + 2, frames, lanes), F32),
            pltpu.VMEM((rows, frames, lanes), F32),
            pltpu.VMEM((rows + 2, 8, lanes), F32),
            pltpu.VMEM((rows, 8, lanes), F32),
            pltpu.VMEM((tall, 8 * (quads - 2), 512), BF),
            pltpu.VMEM(((rows + 2) // 2 * 8 * (quads - 2), 256), F32),
            pltpu.VMEM((nt, fl * rows, own), BF),
            pltpu.VMEM((nt, fl * rows, own), BF),
            pltpu.VMEM((rows, 8 * (own // 256), 256), BF),
            pltpu.SemaphoreType.DMA((count,)),
            pltpu.SemaphoreType.DMA((count,)),
        ],
        compiler_params=pltpu.CompilerParams(
            collective_id=3, has_side_effects=True, vmem_limit_bytes=56 * 2**20
        ),
        name="group",
    )(jnp.pad(cotangent, pads), jnp.pad(saved_pre, pads), jnp.pad(saved_mix, pads), perm, back,
      comb, inner, outer)
    flat = jnp.stack((one, two)).reshape(-1, 128)
    both = reduce_all(flat).reshape((2,) + kernel_one.shape)
    return (grad.reshape(cotangent.shape), both[0], both[1])


def solution(mesh):
    placed = (
        P("tm", "space", None),
        P("tm", "space", None),
        P("tm", "space", None),
        P(),
        P(),
        P(),
        P(),
    )
    return jax.shard_map(
        on_device,
        mesh=mesh,
        in_specs=placed,
        out_specs=(P("tm", "space", None), P(), P()),
        check_vma=False,
    )
```
